32 devices in a mesh: ctx: 8 (over y, x, core), wa: 4 (over z).
Axes of the slice: x: 2, y: 2, z: 4, core: 2. Of those that a mesh axis runs over, the one named last changes fastest.
Arguments:
- block_input: bfloat16 [1024, 1088], P('ctx'), may hold values from -6 to 6
- span_table: int32 [8, 2], replicated, may hold values from 0 to 15, as said below
- doc_ids: int32 [1024], replicated, may hold values from 0 to 3, never falling along the last dimension, each value on 1 to 512 neighbouring positions
- attn_gain: float32 [1088], replicated, may hold values from 0.5 to 1.5
- attn_shift: float32 [1088], replicated, may hold values from -1.75 to 1.75
- qkv_weight: bfloat16 [1088, 3264], P('wa'), may hold values from -0.1875 to 0.1875
- query_bias: float32 [1088], replicated, may hold values from -3 to 3
- value_bias: float32 [1088], replicated, may hold values from -3 to 3
- out_weight: bfloat16 [1088, 1088], P(None, 'wa'), may hold values from -1 to 1
- out_bias: float32 [1088], replicated, may hold values from -3 to 3
- mlp_gain: float32 [1088], replicated, may hold values from 0.1 to 1.9
- mlp_shift: float32 [1088], replicated, may hold values from -1.75 to 1.75
- up_weight: bfloat16 [1088, 4352], P(None, 'wa'), may hold values from -0.1875 to 0.1875
- up_bias: float32 [4352], P('wa'), may hold values from -3 to 3
- down_weight: bfloat16 [4352, 1088], P('wa'), may hold values from -0.09375 to 0.09375
- down_bias: float32 [1088], replicated, may hold values from -6 to 6
- cotangent: bfloat16 [1024, 1088], P('ctx'), may hold values from -6 to 6
Outputs:
- block_output: bfloat16 [1024, 1088], P('ctx', 'wa')
- input_grad: bfloat16 [1024, 1088], P('ctx')
- qkv_grad: float32 [1088, 3264], P('wa', 'ctx')
- query_bias_grad: float32 [1088], replicated
- value_bias_grad: float32 [1088], replicated
- out_grad: float32 [1088, 1088], P('ctx', 'wa')
- out_bias_grad: float32 [1088], replicated
- up_grad: float32 [1088, 4352], P('ctx', 'wa')
- up_bias_grad: float32 [4352], P('wa')
- down_grad: float32 [4352, 1088], P('wa', 'ctx')
- down_bias_grad: float32 [1088], replicated
- attn_gain_grad: float32 [1088], replicated
- attn_shift_grad: float32 [1088], replicated
- mlp_gain_grad: float32 [1088], replicated
- mlp_shift_grad: float32 [1088], replicated
The draws below stay inside these ranges and needn't reach their ends.
Inputs may be any that keep to these rules, and one draw needn't show every extreme that they name: The spans of 64 tokens are numbered in sequence order; the two spans of each row of span_table have numbers that add up to the count of spans minus one, and every span stands in exactly one row. `doc_ids`: document numbers never fall along the sequence; each document holds at most 512 tokens.
All inputs are finite; a program needn't handle non-finite values.
Results may differ from the reference program's by a relative error of at most 0.033.
Values may be sent and summed in bfloat16 or wider, within the bound.
No kernel may reach another device: no remote copies, remote signals or barrier semaphores. Data moves between devices by JAX's collectives and lax.ppermute only.
A program may use at most 320 MiB of HBM per device.

```python
import math
import jax
import jax.numpy as jnp
import numpy as np
from jax import lax

D = 1088
HEADS = 17
HEAD_DIM = 64
FF = 4352
TOK_CTX = 128
TOKENS = 1024
SPAN = 64
DOCS = 4
DOC_MOST = 512


def draw_span_table(key, part):
    pair_count = TOKENS // (2 * SPAN)
    group_count = pair_count // 2
    groups = jax.random.permutation(jax.random.fold_in(key, 11), group_count).astype(jnp.int32)
    group_flips = jax.random.randint(jax.random.fold_in(key, 12), (group_count,), 0, 2, dtype=jnp.int32)
    owner = jnp.arange(pair_count, dtype=jnp.int32)
    member = owner % group_count
    upper = owner // group_count
    order = (2 * groups[member] + upper).astype(jnp.int32)
    flips = group_flips[member]
    mirror = 2 * pair_count - 1 - order
    leading = jnp.where(flips == 1, mirror, order)
    trailing = jnp.where(flips == 1, order, mirror)
    return jnp.stack([leading, trailing], axis=1).astype(jnp.int32)


def strengthened(drawn, rng, source, target, parts, factor):
    owner, partner = [(jnp.arange(drawn.shape[position]) // (drawn.shape[position] // parts)).reshape([-1 if axis == position else 1 for axis in range(drawn.ndim)]) for position in (source, target)]
    chosen = jax.random.permutation(rng, parts)[partner]
    strong = (owner == chosen) | (owner == (partner + parts // 2) % parts)
    return jnp.where(strong, factor * drawn, drawn)


def shard_levels(key, shape, split, smallest, high):
    def one(position, parts):
        draws = jax.random.uniform(jax.random.fold_in(jax.random.fold_in(key, 6), position), (parts,), jnp.float32, smallest / len(split), high / len(split))
        return jnp.repeat(jnp.exp(draws), shape[position] // parts).reshape((-1,) + (1,) * (len(shape) - position - 1))

    factor_of = one(*split[0])
    for cut in split[1:]:
        factor_of = factor_of * one(*cut)
    return factor_of


def split_up(count, total, bound, skew):
    portions = [(1 << 20) // math.isqrt(standing ** skew) + 1 for standing in range(2, count + 1)]
    surplus, counts = total - bound - (count - 1), [1] * (count - 1)
    while surplus > 0:
        movable = [i for i in range(count - 1) if counts[i] < bound]
        whole, remaining = sum([portions[i] for i in movable]), surplus
        for i in movable:
            addition = min(bound - counts[i], max(1, remaining * portions[i] // whole), surplus)
            counts[i] = counts[i] + addition
            surplus = surplus - addition
    return np.array([bound] + counts)


def ragged(own_key, number_of, total, bound, lean):
    if number_of == 2:
        one = jax.random.randint(own_key, (), max(1, total - bound), min(bound, total - 1) + 1)
        return jnp.stack([one, total - one])
    tallies = jnp.asarray(split_up(number_of, total, bound, lean), jnp.int32)
    twos = (number_of - 1) // 2
    source_of, sink = tallies[1:1 + 2 * twos:2], tallies[2:2 + 2 * twos:2]
    slack = jnp.minimum(source_of - 1, bound - sink)
    passed = jax.random.randint(jax.random.fold_in(own_key, 1), (twos,), 0, 1 << 20) % (slack + 1)
    tallies = tallies.at[1:1 + 2 * twos:2].set(source_of - passed).at[2:2 + 2 * twos:2].set(sink + passed)
    return tallies[jax.random.permutation(jax.random.fold_in(own_key, 2), number_of)]


def scatter_about(key, extent, spread, limit, cuts=(), kind=jnp.bfloat16):
    drawn = spread * jax.random.normal(key, extent, jnp.float32)
    if cuts:
        drawn = drawn * shard_levels(key, extent, cuts, -0.22, 0.18)
    return jnp.clip(drawn, -limit, limit).astype(kind)


def gaussian_with(own_key, dims, width, most, cuts, heavy, held_as=jnp.bfloat16):
    drawn = width * jax.random.normal(own_key, dims, jnp.float32)
    if cuts:
        drawn = drawn * shard_levels(own_key, dims, cuts, -0.22, 0.18)
    return jnp.clip(strengthened(drawn, jax.random.fold_in(own_key, 3), *heavy), -most, most).astype(held_as)


def setup_inputs(seed: int = 0) -> dict:
    streams_of = jax.random.split(jax.random.key(seed), 18)
    return {
        "block_input": scatter_about(streams_of[0], (TOKENS, D), 1.0, 6.0, ((0, 8),)),
        "span_table": draw_span_table(jax.random.fold_in(streams_of[17], 71), 0),
        "doc_ids": jnp.searchsorted(jnp.cumsum(ragged(streams_of[2], DOCS, TOKENS, DOC_MOST, 1)), jnp.arange(TOKENS), side="right").astype(jnp.int32),
        "attn_gain": jnp.clip(1.0 + 0.1 * jax.random.normal(streams_of[3], (D,), jnp.float32), 0.5, 1.5),
        "attn_shift": scatter_about(streams_of[4], (D,), 0.3, 1.75, (), jnp.float32),
        "qkv_weight": scatter_about(streams_of[5], (D, 3 * D), D ** -0.5, 0.1875, ((0, 4),)),
        "query_bias": scatter_about(streams_of[6], (D,), 0.5, 3.0, (), jnp.float32),
        "value_bias": scatter_about(streams_of[7], (D,), 0.5, 3.0, (), jnp.float32),
        "out_weight": scatter_about(streams_of[8], (D, D), (max(2, 16 * D // DOC_MOST)) ** -0.5, 1.0, ((1, 4),)),
        "out_bias": scatter_about(streams_of[9], (D,), 0.5, 3.0, (), jnp.float32),
        "mlp_gain": jnp.clip(1.0 + 0.18 * jax.random.normal(streams_of[10], (D,), jnp.float32), 0.1, 1.9),
        "mlp_shift": scatter_about(streams_of[11], (D,), 0.3, 1.75, (), jnp.float32),
        "up_weight": scatter_about(streams_of[12], (D, FF), D ** -0.5, 0.1875, ((1, 4),)),
        "up_bias": scatter_about(streams_of[13], (FF,), 0.5, 3.0, ((0, 4),), jnp.float32),
        "down_weight": scatter_about(streams_of[14], (FF, D), FF ** -0.5, 0.09375, ((0, 4),)),
        "down_bias": scatter_about(streams_of[15], (D,), 1.0, 6.0, (), jnp.float32),
        "cotangent": gaussian_with(streams_of[16], (TOKENS, D), 1.0, 6.0, ((0, 8),), (0, 1, 8, 2.0)),
    }


norm_eps = 1e-05
root_half = 0.7071067811865476
inv_root_tau = 0.3989422804014327

def rounded(value):
    return lax.optimization_barrier(value.astype(jnp.bfloat16))

def gelu_value(pre):
    return 0.5 * pre * (1.0 + lax.erf(pre * root_half))

def gelu_slope(pre):
    return 0.5 * (1.0 + lax.erf(pre * root_half)) + pre * inv_root_tau * jnp.exp(-0.5 * pre * pre)

def norm_parts(values, gain, shift):
    center = lax.optimization_barrier(jnp.mean(values, axis=-1, keepdims=True))
    square = lax.optimization_barrier(jnp.mean(values * values, axis=-1, keepdims=True))
    inv_std = lax.rsqrt(square - center * center + norm_eps)
    normed = (values - center) * inv_std
    return (normed, inv_std, normed * gain + shift)

def norm_back(grad_out, normed, inv_std, gain):
    scaled = grad_out * gain
    return inv_std * (scaled - lax.optimization_barrier(jnp.mean(scaled, axis=-1, keepdims=True)) - normed * lax.optimization_barrier(jnp.mean(scaled * normed, axis=-1, keepdims=True)))

def token_places(row_ids, span_table, doc_ids):
    owner = row_ids // TOK_CTX
    halves = row_ids % TOK_CTX // SPAN
    places = (span_table[owner, halves] * SPAN + row_ids % SPAN).astype(jnp.int32)
    return (places, doc_ids[places])

def reference(block_input, span_table, doc_ids, attn_gain, attn_shift, qkv_weight, query_bias, value_bias, out_weight, out_bias, mlp_gain, mlp_shift, up_weight, up_bias, down_weight, down_bias, cotangent):
    score_scale = float(HEAD_DIM) ** (-0.5)
    row_ids = jnp.arange(TOKENS, dtype=jnp.int32)
    places, docs = token_places(row_ids, span_table, doc_ids)
    input_f = block_input.astype(jnp.float32)
    attn_hat, attn_inv, attn_norm = norm_parts(input_f, attn_gain, attn_shift)
    normed_in = attn_norm.astype(jnp.bfloat16)
    bias_row = jnp.concatenate([query_bias, jnp.zeros_like(query_bias), value_bias])
    qkv_all = rounded(jnp.dot(normed_in, qkv_weight, preferred_element_type=jnp.float32) + bias_row)
    qkv_f = qkv_all.astype(jnp.float32)
    query_heads = qkv_f[:, :D].reshape(TOKENS, HEADS, HEAD_DIM)
    key_heads = qkv_f[:, D:2 * D].reshape(TOKENS, HEADS, HEAD_DIM)
    val_heads = qkv_f[:, 2 * D:].reshape(TOKENS, HEADS, HEAD_DIM)
    block_rows = math.gcd(TOKENS, 512)
    block_count = TOKENS // block_rows

    def split_rows(values):
        return values.reshape((block_count, block_rows) + values.shape[1:])

    def visible(place_block, doc_block):
        return (docs[None, :] == doc_block[:, None]) & (places[None, :] <= place_block[:, None])

    def forward_block(inputs):
        query_block, place_block, doc_block = inputs
        allowed = visible(place_block, doc_block)
        scores = jnp.einsum('qhd,khd->hqk', query_block, key_heads) * score_scale
        scores = jnp.where(allowed[None], scores, -jnp.inf)
        row_top = lax.optimization_barrier(jnp.max(scores, axis=-1, keepdims=True))
        log_block = row_top[..., 0] + jnp.log(lax.optimization_barrier(jnp.sum(jnp.exp(scores - row_top), axis=-1)))
        weights = rounded(jnp.exp(scores - log_block[..., None])).astype(jnp.float32)
        mixed = jnp.einsum('hqk,khd->qhd', weights, val_heads)
        return (mixed, log_block.T)
    mixed_all, log_all = lax.map(forward_block, (split_rows(query_heads), split_rows(places), split_rows(docs)))
    attn_out = rounded(mixed_all.reshape(TOKENS, D))
    log_norm = log_all.reshape(TOKENS, HEADS)
    resid = input_f + jnp.dot(attn_out, out_weight, preferred_element_type=jnp.float32) + out_bias
    mlp_hat, mlp_inv, mlp_norm = norm_parts(resid, mlp_gain, mlp_shift)
    normed_mid = mlp_norm.astype(jnp.bfloat16)
    hidden_pre = jnp.dot(normed_mid, up_weight, preferred_element_type=jnp.float32) + up_bias
    hidden_act = gelu_value(hidden_pre).astype(jnp.bfloat16)
    block_output = (resid + jnp.dot(hidden_act, down_weight, preferred_element_type=jnp.float32) + down_bias).astype(jnp.bfloat16)
    grad_f = cotangent.astype(jnp.float32)
    down_bias_grad = lax.optimization_barrier(jnp.sum(grad_f, axis=0))
    down_grad = jnp.dot(hidden_act.T, cotangent, preferred_element_type=jnp.float32)
    hidden_grad = jnp.dot(cotangent, down_weight.T, preferred_element_type=jnp.float32) * gelu_slope(hidden_pre)
    up_bias_grad = lax.optimization_barrier(jnp.sum(hidden_grad, axis=0))
    hidden_grad_b = hidden_grad.astype(jnp.bfloat16)
    up_grad = jnp.dot(normed_mid.T, hidden_grad_b, preferred_element_type=jnp.float32)
    mid_grad = jnp.dot(hidden_grad_b, up_weight.T, preferred_element_type=jnp.float32)
    mlp_gain_grad = lax.optimization_barrier(jnp.sum(mid_grad * mlp_hat, axis=0))
    mlp_shift_grad = lax.optimization_barrier(jnp.sum(mid_grad, axis=0))
    resid_grad = grad_f + norm_back(mid_grad, mlp_hat, mlp_inv, mlp_gain)
    out_bias_grad = lax.optimization_barrier(jnp.sum(resid_grad, axis=0))
    resid_grad_b = resid_grad.astype(jnp.bfloat16)
    out_grad = jnp.dot(attn_out.T, resid_grad_b, preferred_element_type=jnp.float32)
    attn_grad = rounded(jnp.dot(resid_grad_b, out_weight.T, preferred_element_type=jnp.float32))
    grad_heads = attn_grad.astype(jnp.float32).reshape(TOKENS, HEADS, HEAD_DIM)
    out_heads = attn_out.astype(jnp.float32).reshape(TOKENS, HEADS, HEAD_DIM)
    delta = lax.optimization_barrier(jnp.sum(grad_heads * out_heads, axis=-1))
    log_hi = rounded(log_norm)
    log_lo = rounded(log_norm - log_hi.astype(jnp.float32))
    log_sent = log_hi.astype(jnp.float32) + log_lo.astype(jnp.float32)
    delta_hi = rounded(delta)
    delta_lo = rounded(delta - delta_hi.astype(jnp.float32))
    delta_sent = delta_hi.astype(jnp.float32) + delta_lo.astype(jnp.float32)

    def backward_block(grads, inputs):
        key_acc, val_acc = grads
        query_block, grad_block, log_block, delta_block, place_block, doc_block = inputs
        allowed = visible(place_block, doc_block)
        scores = jnp.einsum('qhd,khd->hqk', query_block, key_heads) * score_scale
        exp_scores = jnp.exp(jnp.where(allowed[None], scores - log_block.T[..., None], -jnp.inf))
        slopes = jnp.einsum('qhd,khd->hqk', grad_block, val_heads)
        score_grad = rounded(exp_scores * (slopes - delta_block.T[..., None])).astype(jnp.float32)
        weights = rounded(exp_scores).astype(jnp.float32)
        query_grad = jnp.einsum('hqk,khd->qhd', score_grad, key_heads) * score_scale
        key_acc = key_acc + jnp.einsum('hqk,qhd->khd', score_grad, query_block)
        val_acc = val_acc + jnp.einsum('hqk,qhd->khd', weights, grad_block)
        return ((key_acc, val_acc), query_grad)
    zero_heads = jnp.zeros((TOKENS, HEADS, HEAD_DIM), jnp.float32)
    sums_kv, query_grads = lax.scan(backward_block, (zero_heads, zero_heads), (split_rows(query_heads), split_rows(grad_heads), split_rows(log_sent), split_rows(delta_sent), split_rows(places), split_rows(docs)))
    key_grad, val_grad = sums_kv
    qkv_grad_b = rounded(jnp.concatenate([query_grads.reshape(TOKENS, D), (key_grad * score_scale).reshape(TOKENS, D), val_grad.reshape(TOKENS, D)], axis=1))
    grad_sums = lax.optimization_barrier(jnp.sum(qkv_grad_b.astype(jnp.float32), axis=0))
    query_bias_grad = grad_sums[:D]
    value_bias_grad = grad_sums[2 * D:]
    qkv_grad = jnp.dot(normed_in.T, qkv_grad_b, preferred_element_type=jnp.float32)
    normed_grad = jnp.dot(qkv_grad_b, qkv_weight.T, preferred_element_type=jnp.float32)
    attn_gain_grad = lax.optimization_barrier(jnp.sum(normed_grad * attn_hat, axis=0))
    attn_shift_grad = lax.optimization_barrier(jnp.sum(normed_grad, axis=0))
    input_grad = (resid_grad + norm_back(normed_grad, attn_hat, attn_inv, attn_gain)).astype(jnp.bfloat16)
    return (block_output, input_grad, qkv_grad, query_bias_grad, value_bias_grad, out_grad, out_bias_grad, up_grad, up_bias_grad, down_grad, down_bias_grad, attn_gain_grad, attn_shift_grad, mlp_gain_grad, mlp_shift_grad)
```

```python
import functools

import jax
import jax.numpy as jnp
import numpy as np
from jax import lax
from jax.experimental import pallas as pl
from jax.experimental.pallas import tpu as pltpu
from jax.sharding import PartitionSpec as P

HEADS = 17
HEAD_DIM = 64
SPAN = 64


norm_eps = 1e-05
root_half = 0.7071067811865476
inv_root_tau = 0.3989422804014327
score_scale = float(HEAD_DIM) ** (-0.5)
masked = -1e30
f32 = jnp.float32
bf16 = jnp.bfloat16


def gelu_value(pre):
    return 0.5 * pre * (1.0 + lax.erf(pre * root_half))


def gelu_slope(pre):
    return 0.5 * (1.0 + lax.erf(pre * root_half)) + pre * inv_root_tau * jnp.exp(-0.5 * pre * pre)


def norm_parts(values, gain, shift):
    center = jnp.mean(values, axis=-1, keepdims=True)
    square = jnp.mean(values * values, axis=-1, keepdims=True)
    inv_std = lax.rsqrt(square - center * center + norm_eps)
    normed = (values - center) * inv_std
    return (normed, inv_std, normed * gain + shift)


def norm_back(grad_out, normed, inv_std, gain):
    scaled = grad_out * gain
    return inv_std * (
        scaled
        - jnp.mean(scaled, axis=-1, keepdims=True)
        - normed * jnp.mean(scaled * normed, axis=-1, keepdims=True)
    )


def dot(left, right, left_dim=1, right_dim=0):
    return lax.dot_general(
        left, right, (((left_dim,), (right_dim,)), ((), ())), preferred_element_type=f32
    )


def group_heads(groups, chunks):
    most = -(-HEADS // groups)
    blocks = 3 * HEADS
    windows = []
    if chunks and (blocks * HEAD_DIM) % chunks == 0:
        width = blocks * HEAD_DIM // chunks
        for c in range(chunks):
            first, last = c * width // HEAD_DIM, (c * width + width - 1) // HEAD_DIM
            windows.append([b % HEADS for b in range(first, last + 1)])
    chosen = [-1] * HEADS

    def fits():
        for group in range(groups):
            if chosen.count(group) > most:
                return False
            for window in windows:
                if sum(chosen[h] == group for h in window) > 2:
                    return False
        return True

    def place(head):
        if head == HEADS:
            return True
        for turn in range(groups):
            chosen[head] = (head + turn) % groups
            if fits() and place(head + 1):
                return True
        chosen[head] = -1
        return False

    if not place(0):
        return None
    lists = [[h for h in range(HEADS) if chosen[h] == g] for g in range(groups)]
    return [heads + [-1] * (most - len(heads)) for heads in lists]


def swap(x, bits):
    count = lax.axis_size("ctx")
    return lax.ppermute(x, "ctx", [(i, i ^ bits) for i in range(count)])


def ctx_gather(x, dim, fast):
    count = lax.axis_size("ctx")
    if not fast:
        return lax.all_gather(x, "ctx", axis=dim, tiled=True)
    me = lax.axis_index("ctx")
    width = x.shape[dim]
    shape = list(x.shape)
    shape[dim] = width * count
    whole = jnp.zeros(shape, x.dtype)
    far = {0: x}
    for bits in (2, 4, 6):
        far[bits] = swap(x, bits)
    for bits in (0, 2, 4, 6):
        far[bits + 1] = swap(far[bits], 1)
    for bits in (0, 1, 2, 4, 6, 3, 5, 7):
        whole = lax.dynamic_update_slice_in_dim(whole, far[bits], (me ^ bits) * width, dim)
    return whole


def ctx_scatter(x, fast):
    if not fast:
        return lax.psum_scatter(x.astype(f32), "ctx", scatter_dimension=0, tiled=False)
    x = x.astype(bf16)
    me = lax.axis_index("ctx")
    core, chip = me & 1, me >> 1
    x = x.reshape((4, 2) + x.shape[1:])
    keep = lax.dynamic_index_in_dim(x, core, 1, False)
    send = lax.dynamic_index_in_dim(x, 1 - core, 1, False)
    both = (keep.astype(f32) + swap(send, 1).astype(f32)).astype(bf16)
    total = lax.dynamic_index_in_dim(both, chip, 0, False).astype(f32)
    parts = [
        swap(lax.dynamic_index_in_dim(both, chip ^ bits, 0, False), 2 * bits) for bits in (1, 2, 3)
    ]
    for part in parts:
        total = total + part.astype(f32)
    return total


def ctx_exchange(x, fast):
    if not fast:
        return lax.all_to_all(x, "ctx", 0, 0)
    me = lax.axis_index("ctx")
    whole = jnp.zeros(x.shape, x.dtype)
    whole = lax.dynamic_update_index_in_dim(
        whole, lax.dynamic_index_in_dim(x, me, 0, False), me, 0
    )
    for bits in (2, 4, 6, 3, 5, 7, 1):
        got = swap(lax.dynamic_index_in_dim(x, me ^ bits, 0, False), bits)
        whole = lax.dynamic_update_index_in_dim(whole, got, me ^ bits, 0)
    return whole


def ctx_sum(x, fast):
    if not fast:
        return lax.psum(x, "ctx")
    for bits in (1, 2, 4):
        x = x + swap(x, bits)
    return x


def wa_shift(x, step):
    count = lax.axis_size("wa")
    return lax.ppermute(x, "wa", [(i, (i + step) % count) for i in range(count)])


def wa_gather(x, dim):
    count = lax.axis_size("wa")
    me = lax.axis_index("wa")
    width = x.shape[dim]
    shape = list(x.shape)
    shape[dim] = width * count
    whole = jnp.zeros(shape, x.dtype)
    whole = lax.dynamic_update_slice_in_dim(whole, x, me * width, dim)
    for step in range(1, count):
        got = wa_shift(x, step)
        owner = (me + count - step) % count
        whole = lax.dynamic_update_slice_in_dim(whole, got, owner * width, dim)
    return whole


def wa_exchange(x):
    count = lax.axis_size("wa")
    me = lax.axis_index("wa")
    whole = jnp.zeros(x.shape, x.dtype)
    whole = lax.dynamic_update_index_in_dim(
        whole, lax.dynamic_index_in_dim(x, me, 0, False), me, 0
    )
    for step in range(1, count):
        got = wa_shift(lax.dynamic_index_in_dim(x, (me + step) % count, 0, False), step)
        whole = lax.dynamic_update_index_in_dim(whole, got, (me + count - step) % count, 0)
    return whole


def wa_scatter(x):
    count = lax.axis_size("wa")
    me = lax.axis_index("wa")
    sent = x.astype(bf16)
    total = lax.dynamic_index_in_dim(x, me, 0, False).astype(f32)
    parts = [
        wa_shift(lax.dynamic_index_in_dim(sent, (me + step) % count, 0, False), step)
        for step in range(1, count)
    ]
    for part in parts:
        total = total + part.astype(f32)
    return total


def wa_sum(x):
    parts = [wa_shift(x, step) for step in range(1, lax.axis_size("wa"))]
    for part in parts:
        x = x + part
    return x


def head_cols(part, head, per):
    start = (part * per + head) * HEAD_DIM
    return pl.ds(start, HEAD_DIM)


def attend_kernel(per, own_ref, qrow_ref, krow_ref, qkv_ref, out_ref, log_ref):
    rows = out_ref.shape[0]
    mine = pl.ds(pl.multiple_of(own_ref[0] * rows, rows), rows)
    allowed = (qrow_ref[:, 1:2] == krow_ref[1:2, :]) & (krow_ref[0:1, :] <= qrow_ref[:, 0:1])
    logs = []
    for head in range(per):
        query = qkv_ref[mine, head_cols(0, head, per)]
        key = qkv_ref[:, head_cols(1, head, per)]
        value = qkv_ref[:, head_cols(2, head, per)]
        scores = jnp.where(allowed, dot(query, key, 1, 1) * score_scale, masked)
        top = jnp.max(scores, axis=1, keepdims=True)
        weights = jnp.exp(scores - top)
        total = jnp.sum(weights, axis=1, keepdims=True)
        mixed = dot(weights.astype(bf16), value) / total
        out_ref[:, pl.ds(head * HEAD_DIM, HEAD_DIM)] = mixed.astype(bf16)
        logs.append(top + jnp.log(total))
    log_ref[...] = jnp.concatenate(logs, axis=1)


def grads_kernel(per, group_ref, resid_ref, weight_ref, out_ref, log_ref, pack_ref):
    width = per * HEAD_DIM
    mine = pl.ds(pl.multiple_of(group_ref[0] * width, width), width)
    pack_grads(per, dot(resid_ref[...], weight_ref[mine, :], 1, 1), out_ref, log_ref, pack_ref)


def pack_grads(per, grad, out_ref, log_ref, pack_ref):
    width = per * HEAD_DIM
    grad = grad.astype(bf16)
    prod = grad.astype(f32) * out_ref[...].astype(f32)
    delta = jnp.concatenate(
        [
            jnp.sum(prod[:, h * HEAD_DIM : (h + 1) * HEAD_DIM], axis=1, keepdims=True)
            for h in range(per)
        ],
        axis=1,
    )
    logs = log_ref[...]
    log_hi = logs.astype(bf16)
    log_lo = (logs - log_hi.astype(f32)).astype(bf16)
    delta_hi = delta.astype(bf16)
    delta_lo = (delta - delta_hi.astype(f32)).astype(bf16)
    pack_ref[:, :width] = grad
    stats = jnp.concatenate([t.astype(f32) for t in (log_hi, log_lo, delta_hi, delta_lo)], axis=1)
    rest = pack_ref.shape[1] - width - 4 * per
    pad = jnp.zeros((grad.shape[0], rest), f32)
    pack_ref[:, width:] = jnp.concatenate([stats, pad], axis=1).astype(bf16)


def query_back_kernel(per, own_ref, qrow_ref, krow_ref, qkv_ref, pack_ref, grad_ref):
    rows = pack_ref.shape[0]
    width = per * HEAD_DIM
    mine = pl.ds(pl.multiple_of(own_ref[0] * rows, rows), rows)
    allowed = (qrow_ref[:, 1:2] == krow_ref[1:2, :]) & (krow_ref[0:1, :] <= qrow_ref[:, 0:1])
    stats = pack_ref[:, width:].astype(f32)
    for head in range(per):
        query = qkv_ref[mine, head_cols(0, head, per)]
        key = qkv_ref[:, head_cols(1, head, per)]
        value = qkv_ref[:, head_cols(2, head, per)]
        grad = pack_ref[:, pl.ds(head * HEAD_DIM, HEAD_DIM)]
        log = stats[:, head : head + 1] + stats[:, per + head : per + head + 1]
        delta = stats[:, 2 * per + head : 2 * per + head + 1]
        delta = delta + stats[:, 3 * per + head : 3 * per + head + 1]
        scores = jnp.where(allowed, dot(query, key, 1, 1) * score_scale - log, masked)
        slope = (jnp.exp(scores) * (dot(grad, value, 1, 1) - delta)).astype(bf16)
        grad_ref[:, pl.ds(head * HEAD_DIM, HEAD_DIM)] = (dot(slope, key) * score_scale).astype(bf16)


def key_back_kernel(per, own_ref, krow_ref, qrow_ref, qkv_ref, pack_ref, key_ref, value_ref):
    rows = key_ref.shape[0]
    width = per * HEAD_DIM
    mine = pl.ds(pl.multiple_of(own_ref[0] * rows, rows), rows)
    allowed = (krow_ref[:, 1:2] == qrow_ref[1:2, :]) & (krow_ref[:, 0:1] <= qrow_ref[0:1, :])
    stats = jnp.transpose(pack_ref[:, width:].astype(f32))
    for head in range(per):
        query = qkv_ref[:, head_cols(0, head, per)]
        key = qkv_ref[mine, head_cols(1, head, per)]
        value = qkv_ref[mine, head_cols(2, head, per)]
        grad = pack_ref[:, pl.ds(head * HEAD_DIM, HEAD_DIM)]
        log = stats[head : head + 1, :] + stats[per + head : per + head + 1, :]
        delta = stats[2 * per + head : 2 * per + head + 1, :]
        delta = delta + stats[3 * per + head : 3 * per + head + 1, :]
        scores = jnp.where(allowed, dot(key, query, 1, 1) * score_scale - log, masked)
        probs = jnp.exp(scores)
        slope = (probs * (dot(value, grad, 1, 1) - delta)).astype(bf16)
        cols = pl.ds(head * HEAD_DIM, HEAD_DIM)
        key_ref[:, cols] = (dot(slope, query) * score_scale).astype(bf16)
        value_ref[:, cols] = dot(probs.astype(bf16), grad).astype(bf16)


def call(kernel, scalars, arrays, outs, name, scratch=()):
    whole = pl.BlockSpec(memory_space=pltpu.VMEM)
    return pl.pallas_call(
        kernel,
        out_shape=outs,
        in_specs=[pl.BlockSpec(memory_space=pltpu.SMEM)] * len(scalars) + [whole] * len(arrays),
        out_specs=jax.tree.map(lambda _: whole, outs),
        scratch_shapes=list(scratch),
        name=name,
        compiler_params=pltpu.CompilerParams(vmem_limit_bytes=60 * 1024 * 1024),
    )(*scalars, *arrays)


def shifted(wa, step, count):
    return lax.rem(wa + count + step, count)


def prep_kernel(plan, idx_ref, qkv_ref, out_ref, *refs):
    lists, blocks, count = plan
    sends, part_ref, hold = refs[:count], refs[count], refs[count + 1]
    heads_flat = [h for heads in lists for h in heads]
    ctx, wa = idx_ref[0], idx_ref[1]
    rows = qkv_ref.shape[0]
    part = part_ref.shape[0]
    for c in range(8):

        @pl.when(ctx == c)
        def _():
            for g in range(count):
                for i in range(2):
                    b = blocks[g][2 * c + i]
                    cols = slice(i * HEAD_DIM, (i + 1) * HEAD_DIM)
                    if b < 3 * HEADS:
                        hold[g, :, cols] = qkv_ref[:, b * HEAD_DIM : (b + 1) * HEAD_DIM]
                    else:
                        hold[g, :, cols] = jnp.zeros((rows, HEAD_DIM), bf16)
            for k in range(part // 32):
                row = part * c + 32 * k
                head, off = heads_flat[row // HEAD_DIM], row % HEAD_DIM
                if head >= 0:
                    start = head * HEAD_DIM + off
                    part_ref[32 * k : 32 * k + 32, :] = out_ref[start : start + 32, :]
                else:
                    part_ref[32 * k : 32 * k + 32, :] = jnp.zeros((32, out_ref.shape[1]), bf16)

    for s in range(count):
        sends[s][...] = hold[shifted(wa, s, count)]


def stack_rows_kernel(idx_ref, *refs):
    pieces, out_ref = refs[:-1], refs[-1]
    count, rows = len(pieces), pieces[0].shape[0]
    for s in range(count):
        start = pl.multiple_of(shifted(idx_ref[1], -s, count) * rows, rows)
        out_ref[pl.ds(start, rows), :] = pieces[s][...]


def stack_cols_kernel(idx_ref, *refs):
    pieces, out_ref, hold = refs[:-2], refs[-2], refs[-1]
    count, cols = len(pieces), pieces[0].shape[1]
    for s in range(count):
        hold[shifted(idx_ref[1], -s, count)] = pieces[s][...]
    for g in range(count):
        out_ref[:, g * cols : (g + 1) * cols] = hold[g]


def norm_all_kernel(idx_ref, gain_ref, shift_ref, *refs):
    pieces, out_ref = refs[:8], refs[8]
    rows = pieces[0].shape[0]
    for bits in range(8):
        start = pl.multiple_of((idx_ref[0] ^ bits) * rows, rows)
        normed = norm_parts(pieces[bits][...].astype(f32), gain_ref[...], shift_ref[...])[2]
        out_ref[pl.ds(start, rows), :] = normed.astype(bf16)


def front_kernel(per, idx_ref, qrow_ref, krow_ref, bias_ref, normed_ref, *refs):
    pieces = refs[:8]
    qkv_ref, out_ref, log_ref, weight_ref = refs[8:]
    cols = pieces[0].shape[1]
    for bits in range(8):
        start = pl.multiple_of((idx_ref[0] ^ bits) * cols, cols)
        weight_ref[:, pl.ds(start, cols)] = pieces[bits][...]
    tokens = normed_ref.shape[0]
    for row in range(0, tokens, 256):
        part = dot(normed_ref[row : row + 256, :], weight_ref[...]) + bias_ref[...]
        qkv_ref[row : row + 256, :] = part.astype(bf16)
    attend_kernel(per, idx_ref, qrow_ref, krow_ref, qkv_ref, out_ref, log_ref)


def mlp_kernel(count, idx_ref, x_ref, out_bias_ref, gain_ref, shift_ref, up_ref, up_bias_ref, down_ref, down_bias_ref, cot_ref, *refs):
    attn, outs8, refs = refs[:count], refs[count : count + 8], refs[count + 8 :]
    mid_ref, grad_ref, act_ref, own_ref = refs[:4]
    sends, refs = refs[4 : 3 + count], refs[3 + count :]
    hat_ref, inv_ref, cols_ref, sum_ref, group_ref, weight, hold, hats, invs = refs
    ctx, wa = idx_ref[0], idx_ref[1]
    part = outs8[0].shape[0]
    for bits in range(8):
        weight[pl.ds(pl.multiple_of((ctx ^ bits) * part, part), part), :] = outs8[bits][...]
    group = attn[0].shape[1]
    resid = x_ref[...].astype(f32) + out_bias_ref[...]
    for s in range(count):
        start = pl.multiple_of(shifted(wa, -s, count) * group, group)
        resid = resid + dot(attn[s][...], weight[pl.ds(start, group), :])
    group_ref[...] = weight[pl.ds(pl.multiple_of(wa * group, group), group), :]
    hat, inv, norm = norm_parts(resid, gain_ref[...], shift_ref[...])
    hats[...] = hat
    invs[...] = inv
    cols = cols_ref.shape[1]
    for g in range(count):

        @pl.when(wa == g)
        def _():
            span = slice(g * cols, (g + 1) * cols)
            cols_ref[...] = resid[:, span] + down_bias_ref[:, span]

    normed_mid = norm.astype(bf16)
    mid_ref[...] = normed_mid
    pre = dot(normed_mid, up_ref[...]) + up_bias_ref[...]
    phi = 0.5 * (1.0 + lax.erf(pre * root_half))
    act_ref[...] = (pre * phi).astype(bf16)
    slope = phi + pre * inv_root_tau * jnp.exp(-0.5 * pre * pre)
    hidden = dot(cot_ref[...], down_ref[...], 1, 1) * slope
    sum_ref[...] = jnp.sum(hidden, axis=0, keepdims=True)
    hidden_b = hidden.astype(bf16)
    grad_ref[...] = hidden_b
    hold[...] = dot(hidden_b, up_ref[...], 1, 1)
    rows = own_ref.shape[0]
    mine = pl.ds(pl.multiple_of(wa * rows, rows), rows)
    own_ref[...] = hold[mine, :]
    hat_ref[...] = hats[mine, :]
    inv_ref[...] = invs[mine, :]
    for s in range(1, count):
        start = pl.multiple_of(shifted(wa, s, count) * rows, rows)
        sends[s - 1][...] = hold[pl.ds(start, rows), :].astype(bf16)


def weight_grad_kernel(count, idx_ref, mid_ref, grad_ref, act_ref, cot_ref, down_ref, keep_ref, send_ref, *refs):
    outs, hold, cols_hold = refs[:count], refs[count], refs[count + 1]
    core = idx_ref[0] & 1
    rows = keep_ref.shape[2]
    for k, (left, right) in enumerate(((mid_ref, grad_ref), (cot_ref, act_ref))):
        whole = dot(left[...], right[...], 0, 0)
        for j in range(8):
            hold[j % 2, j // 2, k] = whole[j * rows : (j + 1) * rows, :].astype(bf16)
    keep_ref[...] = hold[core]
    send_ref[...] = hold[1 - core]
    down = dot(act_ref[...], down_ref[...])
    cols = outs[0].shape[1]
    for g in range(count):
        cols_hold[g] = down[:, g * cols : (g + 1) * cols]
    for s in range(count):
        outs[s][...] = cols_hold[shifted(idx_ref[1], s, count)].astype(outs[s].dtype)


def pair_sum_kernel(idx_ref, keep_ref, got_ref, own_ref, *sends):
    chip = idx_ref[0] >> 1
    for bits in range(4):
        both = keep_ref[chip ^ bits].astype(f32) + got_ref[chip ^ bits].astype(f32)
        if bits:
            sends[bits - 1][...] = both.astype(bf16)
        else:
            own_ref[...] = both


def out_grad_kernel(plan, idx_ref, *refs):
    lists, count = plan
    attn = refs[:count]
    resid_ref, keep_ref, send_ref, cols_hold, group_hold, hold = refs[count:]
    core, wa = idx_ref[0] & 1, idx_ref[1]
    cols = cols_hold.shape[1]
    for g in range(count):

        @pl.when(wa == g)
        def _():
            cols_hold[...] = resid_ref[:, g * cols : (g + 1) * cols]

    for s in range(count):
        group_hold[shifted(wa, -s, count)] = dot(attn[s][...], cols_hold[...], 0, 0)
    parts = []
    for h in range(HEADS):
        g = next(g for g in range(count) if h in lists[g])
        i = lists[g].index(h)
        parts.append(group_hold[g, i * HEAD_DIM : (i + 1) * HEAD_DIM, :])
    whole = jnp.concatenate(parts, axis=0)
    rows = keep_ref.shape[1]
    for j in range(8):
        hold[j % 2, j // 2] = whole[j * rows : (j + 1) * rows, :].astype(bf16)
    keep_ref[...] = hold[core]
    send_ref[...] = hold[1 - core]


def resid_kernel(count, idx_ref, own_ref, *refs):
    got, refs = refs[: count - 1], refs[count - 1 :]
    hat_ref, inv_ref, cot_ref, gain_ref, grad_ref, grad_b_ref, sums_ref = refs
    mid = own_ref[...]
    for part in got:
        mid = mid + part[...].astype(f32)
    rows = mid.shape[0]
    cot = cot_ref[pl.ds(pl.multiple_of(idx_ref[1] * rows, rows), rows), :].astype(f32)
    hat = hat_ref[...]
    grad = cot + norm_back(mid, hat, inv_ref[...], gain_ref[...])
    grad_ref[...] = grad
    grad_b_ref[...] = grad.astype(bf16)
    sums = [jnp.sum(t, axis=0, keepdims=True) for t in (mid * hat, mid, grad, cot)]
    sums_ref[...] = jnp.concatenate(sums, axis=0)


def pack_kernel(per, count, idx_ref, *refs):
    pieces = refs[:count]
    weight_ref, out_ref, log_ref, resid_ref, pack_ref = refs[count:]
    stack_rows_kernel(idx_ref, *pieces, resid_ref)
    pack_grads(per, dot(resid_ref[...], weight_ref[...], 1, 1), out_ref, log_ref, pack_ref)


def back_kernel(per, count, idx_ref, table_ref, krow_ref, qrow_ref, x_ref, qkv_ref, weight_ref, query_grad_ref, *refs):
    packs, refs = refs[:8], refs[8:]
    own_ref, sends, refs = refs[0], refs[1:count], refs[count:]
    outgoing, refs = refs[:8], refs[8:]
    late_ref, cols_ref, pack_all, grads, keys, values, blocks, hold = refs
    ctx, wa = idx_ref[0], idx_ref[1]
    rows = x_ref.shape[0]
    width = per * HEAD_DIM
    for bits in range(8):
        start = pl.multiple_of((ctx ^ bits) * rows, rows)
        pack_all[pl.ds(start, rows), :] = packs[bits][...]
    key_back_kernel(
        per,
        idx_ref,
        krow_ref,
        qrow_ref,
        qkv_ref,
        pack_all,
        keys,
        values,
    )
    grads[:, width : 2 * width] = keys[...]
    grads[:, 2 * width : 3 * width] = values[...]
    grads[:, :width] = query_grad_ref[...]
    grads[:, 3 * width :] = jnp.zeros((rows, grads.shape[1] - 3 * width), bf16)
    for j in range(grads.shape[1] // HEAD_DIM):
        blocks[j] = grads[:, j * HEAD_DIM : (j + 1) * HEAD_DIM]
    for bits in range(8):
        at = (wa * 8 + (ctx ^ bits)) * 2
        for i in range(2):
            cols = slice(i * HEAD_DIM, (i + 1) * HEAD_DIM)
            outgoing[bits][:, cols] = blocks[table_ref[at + i]]
    cols_ref[...] = jnp.sum(grads[...].astype(f32), axis=0, keepdims=True)
    normed = dot(grads[...], weight_ref[...], 1, 1)
    hold[...] = normed
    hat = norm_parts(x_ref[...].astype(f32), 1.0, 0.0)[0]
    late_ref[...] = jnp.concatenate(
        [jnp.sum(normed * hat, axis=0, keepdims=True), jnp.sum(normed, axis=0, keepdims=True)]
    )
    share = own_ref.shape[0]
    own_ref[...] = hold[pl.ds(pl.multiple_of(wa * share, share), share), :]
    for s in range(1, count):
        start = pl.multiple_of(shifted(wa, s, count) * share, share)
        sends[s - 1][...] = hold[pl.ds(start, share), :].astype(bf16)


def input_grad_kernel(count, idx_ref, own_ref, *refs):
    got, refs = refs[: count - 1], refs[count - 1 :]
    resid_ref, x_ref, gain_ref, out_ref = refs
    grad = own_ref[...]
    for part in got:
        grad = grad + part[...].astype(f32)
    rows = grad.shape[0]
    mine = x_ref[pl.ds(pl.multiple_of(idx_ref[1] * rows, rows), rows), :].astype(f32)
    hat, inv, _ = norm_parts(mine, 1.0, 0.0)
    out_ref[...] = (resid_ref[...] + norm_back(grad, hat, inv, gain_ref[...])).astype(bf16)


def qkv_grad_kernel(count, idx_ref, normed_ref, *refs):
    pieces, sends, hold, turned = refs[:8], refs[8 : 8 + count], refs[-2], refs[-1]
    rows = pieces[0].shape[0]
    for bits in range(8):
        start = pl.multiple_of((idx_ref[0] ^ bits) * rows, rows)
        hold[pl.ds(start, rows), :] = pieces[bits][...]
    turned[...] = jnp.transpose(dot(hold[...], normed_ref[...], 0, 0))
    part = sends[0].shape[0]
    for s in range(count):
        start = pl.multiple_of(shifted(idx_ref[1], s, count) * part, part)
        sends[s][...] = turned[pl.ds(start, part), :].astype(bf16)


def qkv_place_kernel(count, span, idx_ref, order_ref, *refs):
    pieces, out_ref, blocks, line = refs[:count], refs[count], refs[count + 1], refs[count + 2]
    for s in range(count):
        g = shifted(idx_ref[1], -s, count)
        for i in range(2):
            blocks[2 * g + i] = pieces[s][:, i * HEAD_DIM : (i + 1) * HEAD_DIM].astype(f32)
    for j in range(span):
        cols = slice(j * HEAD_DIM, (j + 1) * HEAD_DIM)
        line[:, cols] = blocks[order_ref[idx_ref[0] * 8 + j]]
    chunk = out_ref.shape[1]
    for c in range(8):

        @pl.when(idx_ref[0] == c)
        def _():
            off = c * chunk % HEAD_DIM
            out_ref[...] = line[:, off : off + chunk]


def ctx_pieces(x):
    got = {0: x}
    for bits in (2, 4, 6):
        got[bits] = swap(x, bits)
    for bits in (0, 2, 4, 6):
        got[bits + 1] = swap(got[bits], 1)
    return [got[bits] for bits in range(8)]


def wa_pieces(x):
    return [x] + [wa_shift(x, step) for step in range(1, lax.axis_size("wa"))]


def wa_trade(sends):
    return [sends[0]] + [wa_shift(sends[step], step) for step in range(1, len(sends))]


def chips_sum(keep, send, idx):
    got = swap(send, 1)
    part = jax.ShapeDtypeStruct(keep.shape[1:], bf16)
    own, *sends = call(
        pair_sum_kernel,
        (idx,),
        (keep, got),
        (jax.ShapeDtypeStruct(keep.shape[1:], f32), part, part, part),
        "pair_sum",
    )
    for bits in (1, 2, 3):
        own = own + swap(sends[bits - 1], 2 * bits).astype(f32)
    return own


def body_eight(
    block_input,
    span_table,
    doc_ids,
    attn_gain,
    attn_shift,
    qkv_weight,
    query_bias,
    value_bias,
    out_weight,
    out_bias,
    mlp_gain,
    mlp_shift,
    up_weight,
    up_bias,
    down_weight,
    down_bias,
    cotangent,
):
    rows, width = block_input.shape
    count = lax.axis_size("wa")
    ctx = lax.axis_index("ctx")
    wa = lax.axis_index("wa")
    idx = jnp.stack([ctx, wa]).astype(jnp.int32)
    tokens = rows * 8
    share = rows // count
    cols = width // count
    lists = group_heads(count, 8)
    per = len(lists[0])
    group = per * HEAD_DIM
    slots = 16
    none = 3 * HEADS
    blocks = np.full((count, slots), none, np.int32)
    for g in range(count):
        for part in range(3):
            for i, head in enumerate(lists[g]):
                if head >= 0:
                    blocks[g, part * per + i] = part * HEADS + head

    def shape(*dims, kind=bf16):
        return jax.ShapeDtypeStruct(dims, kind)

    def vmem(*dims, kind=bf16):
        return pltpu.VMEM(dims, kind)

    def row(values):
        return values.reshape(1, -1)

    x_pieces = ctx_pieces(block_input)
    part = count * group // 8
    *sends, out_part = call(
        functools.partial(prep_kernel, (lists, blocks.tolist(), count)),
        (idx,),
        (qkv_weight, out_weight),
        (shape(cols, 2 * HEAD_DIM),) * count + (shape(part, cols),),
        "prep",
        [vmem(count, cols, 2 * HEAD_DIM)],
    )
    piece = call(
        stack_rows_kernel, (idx,), wa_trade(sends), shape(width, 2 * HEAD_DIM), "stack_weight"
    )
    weight_pieces = ctx_pieces(piece)
    out_piece = call(
        stack_cols_kernel,
        (idx,),
        wa_pieces(out_part),
        shape(part, width),
        "stack_out",
        [vmem(count, part, cols)],
    )
    out_pieces = ctx_pieces(out_piece)

    starts = span_table.reshape(-1)
    places = (starts[:, None] * SPAN + jnp.arange(SPAN, dtype=jnp.int32)[None, :]).reshape(-1)
    spans = starts.shape[0]
    pick = starts[:, None] == jnp.arange(spans, dtype=jnp.int32)[None, :]
    docs = jnp.sum(
        jnp.where(pick[:, :, None], doc_ids.reshape(1, spans, SPAN), 0), axis=1, dtype=jnp.int32
    ).reshape(-1)
    where_row = jnp.stack([places, docs])
    own_cols = lax.dynamic_slice_in_dim(where_row, ctx * rows, rows, 1).T
    bias_blocks = jnp.concatenate(
        [
            query_bias.reshape(HEADS, HEAD_DIM),
            jnp.zeros((HEADS, HEAD_DIM), f32),
            value_bias.reshape(HEADS, HEAD_DIM),
            jnp.zeros((1, HEAD_DIM), f32),
        ]
    )
    chosen = (jnp.asarray(blocks)[wa][:, None] == jnp.arange(none + 1)[None, :]).astype(f32)
    group_bias = jnp.sum(chosen[:, :, None] * bias_blocks[None], axis=1).reshape(1, -1)

    normed_all = call(
        norm_all_kernel,
        (idx,),
        (row(attn_gain), row(attn_shift), *x_pieces),
        shape(tokens, width),
        "norm_all",
    )
    qkv_all, attn_out, log_norm, weight = call(
        functools.partial(front_kernel, per),
        (idx,),
        (own_cols, where_row, group_bias, normed_all, *weight_pieces),
        (
            shape(tokens, slots * HEAD_DIM),
            shape(rows, group),
            shape(rows, per, kind=f32),
            shape(width, slots * HEAD_DIM),
        ),
        "front",
    )
    attn = wa_pieces(attn_out)
    mlp_out = call(
        functools.partial(mlp_kernel, count),
        (idx,),
        (
            block_input,
            row(out_bias),
            row(mlp_gain),
            row(mlp_shift),
            up_weight,
            row(up_bias),
            down_weight,
            row(down_bias),
            cotangent,
            *attn,
            *out_pieces,
        ),
        (shape(rows, width),) * 3
        + (shape(share, width, kind=f32),)
        + (shape(share, width),) * (count - 1)
        + (
            shape(share, width, kind=f32),
            shape(share, 1, kind=f32),
            shape(rows, cols, kind=f32),
            shape(1, width, kind=f32),
            shape(group, width),
        ),
        "mlp",
        [
            vmem(count * group, width),
            vmem(rows, width, kind=f32),
            vmem(rows, width, kind=f32),
            vmem(rows, 1, kind=f32),
        ],
    )
    normed_mid, hidden_grad, hidden_act = mlp_out[:3]
    mid = wa_trade(mlp_out[3 : 3 + count])
    hat_share, inv_share, resid_cols, up_sum, out_group = mlp_out[3 + count :]
    resid_grad, resid_b, early = call(
        functools.partial(resid_kernel, count),
        (idx,),
        (*mid, hat_share, inv_share, cotangent, row(mlp_gain)),
        (shape(share, width, kind=f32), shape(share, width), shape(4, width, kind=f32)),
        "resid_back",
    )
    keep, send, *down_sends = call(
        functools.partial(weight_grad_kernel, count),
        (idx,),
        (normed_mid, hidden_grad, hidden_act, cotangent, down_weight),
        (shape(4, 2, width // 8, width),) * 2
        + (shape(rows, cols, kind=f32),)
        + (shape(rows, cols),) * (count - 1),
        "weight_grad",
        [vmem(2, 4, 2, width // 8, width), vmem(count, rows, cols, kind=f32)],
    )
    both_grads = chips_sum(keep, send, idx)
    up_grad, down_grad = both_grads[0], both_grads[1].T
    total = resid_cols
    for got in wa_trade(down_sends):
        total = total + got.astype(f32)
    block_output = total.astype(bf16)

    resid_full, pack = call(
        functools.partial(pack_kernel, per, count),
        (idx,),
        (*wa_pieces(resid_b), out_group, attn_out, log_norm),
        (shape(rows, width), shape(rows, -(-(group + 4 * per) // 128) * 128)),
        "pack",
    )
    pack_pieces = ctx_pieces(pack)
    query_grad = call(
        functools.partial(query_back_kernel, per),
        (idx,),
        (own_cols, where_row, qkv_all, pack),
        shape(rows, group),
        "query_back",
    )
    keep, send = call(
        functools.partial(out_grad_kernel, (lists, count)),
        (idx,),
        (*attn, resid_full),
        (shape(4, width // 8, cols),) * 2,
        "out_grad",
        [
            vmem(rows, cols),
            vmem(count, group, cols, kind=f32),
            vmem(2, 4, width // 8, cols),
        ],
    )
    out_grad = chips_sum(keep, send, idx)

    chunk = 3 * width // 8
    table = np.full((count, 8, 2), slots - 1, np.int32)
    order = np.zeros((8, 8), np.int32)
    span = 0
    for c in range(8):
        used = [0] * count
        first, last = c * chunk // HEAD_DIM, (c * chunk + chunk - 1) // HEAD_DIM
        span = max(span, last - first + 1)
        for b in range(first, last + 1):
            g = next(g for g in range(count) if b % HEADS in lists[g])
            table[g, c, used[g]] = (b // HEADS) * per + lists[g].index(b % HEADS)
            order[c, b - first] = 2 * g + used[g]
            used[g] += 1
    back = call(
        functools.partial(back_kernel, per, count),
        (idx, jnp.asarray(table.reshape(-1))),
        (own_cols, where_row, block_input, qkv_all, weight, query_grad, *pack_pieces),
        (shape(share, width, kind=f32),)
        + (shape(share, width),) * (count - 1)
        + (shape(rows, 2 * HEAD_DIM),) * 8
        + (shape(2, width, kind=f32), shape(1, slots * HEAD_DIM, kind=f32)),
        "back",
        [
            vmem(tokens, pack.shape[1]),
            vmem(rows, slots * HEAD_DIM),
            vmem(rows, group),
            vmem(rows, group),
            vmem(slots, rows, HEAD_DIM),
            vmem(rows, width, kind=f32),
        ],
    )
    input_share = call(
        functools.partial(input_grad_kernel, count),
        (idx,),
        (*wa_trade(back[:count]), resid_grad, block_input, row(attn_gain)),
        shape(share, width),
        "input_back",
    )
    input_grad = call(
        stack_rows_kernel, (idx,), wa_pieces(input_share), shape(rows, width), "stack_input"
    )
    outgoing = back[count : count + 8]
    late, col_sums = back[count + 8 :]
    columns = [outgoing[0]] + [None] * 7
    for bits in (2, 4, 6, 3, 5, 7, 1):
        columns[bits] = swap(outgoing[bits], bits)
    found = call(
        functools.partial(qkv_grad_kernel, count),
        (idx,),
        (normed_all, *columns),
        (shape(cols, 2 * HEAD_DIM),) * count,
        "qkv_grad",
        [vmem(tokens, 2 * HEAD_DIM), vmem(width, 2 * HEAD_DIM, kind=f32)],
    )
    qkv_grad = call(
        functools.partial(qkv_place_kernel, count, span),
        (idx, jnp.asarray(order.reshape(-1))),
        wa_trade(found),
        shape(cols, chunk, kind=f32),
        "qkv_place",
        [vmem(2 * count, cols, HEAD_DIM, kind=f32), vmem(cols, 8 * HEAD_DIM, kind=f32)],
    )
    all_sums = jnp.sum(chosen[:, :, None] * col_sums.reshape(slots, 1, HEAD_DIM), axis=0)
    sums = jnp.concatenate(
        [
            late,
            row(all_sums[:HEADS]),
            row(all_sums[2 * HEADS : 3 * HEADS]),
            early,
            up_sum,
        ]
    )
    sums = ctx_sum(sums, True)
    up_bias_grad = sums[8]
    sums = wa_sum(sums[:8])
    return (
        block_output,
        input_grad,
        qkv_grad,
        sums[2],
        sums[3],
        out_grad,
        sums[6],
        up_grad,
        up_bias_grad,
        down_grad,
        sums[7],
        sums[0],
        sums[1],
        sums[4],
        sums[5],
    )


def body(
    fast,
    block_input,
    span_table,
    doc_ids,
    attn_gain,
    attn_shift,
    qkv_weight,
    query_bias,
    value_bias,
    out_weight,
    out_bias,
    mlp_gain,
    mlp_shift,
    up_weight,
    up_bias,
    down_weight,
    down_bias,
    cotangent,
):
    rows, width = block_input.shape
    ctx_count = lax.axis_size("ctx")
    wa_count = lax.axis_size("wa")
    ctx = lax.axis_index("ctx")
    wa = lax.axis_index("wa")
    tokens = rows * ctx_count
    part_rows = rows // wa_count
    col_width = width // wa_count
    lists = group_heads(wa_count, ctx_count if fast else 0)
    per = len(lists[0])
    group_width = per * HEAD_DIM
    slots = 2 * ctx_count if fast else 3 * per
    none = 3 * HEADS
    blocks = np.full((wa_count, slots), none, np.int32)
    for g in range(wa_count):
        for part in range(3):
            for i, head in enumerate(lists[g]):
                if head >= 0:
                    blocks[g, part * per + i] = part * HEADS + head
    heads_flat = [h for heads in lists for h in heads]

    starts = span_table.reshape(-1)
    places = (starts[:, None] * SPAN + jnp.arange(SPAN, dtype=jnp.int32)[None, :]).reshape(-1)
    spans = starts.shape[0]
    pick = starts[:, None] == jnp.arange(spans, dtype=jnp.int32)[None, :]
    docs = jnp.sum(
        jnp.where(pick[:, :, None], doc_ids.reshape(1, spans, SPAN), 0), axis=1, dtype=jnp.int32
    ).reshape(-1)
    where_row = jnp.stack([places, docs])
    own_cols = lax.dynamic_slice_in_dim(where_row, ctx * rows, rows, 1).T

    own_ctx = ctx.reshape(1).astype(jnp.int32)
    own_wa = wa.reshape(1).astype(jnp.int32)

    def column_block(matrix, block):
        got = lax.dynamic_slice_in_dim(matrix, jnp.minimum(block, none - 1) * HEAD_DIM, HEAD_DIM, 1)
        return jnp.where(block < none, got, jnp.zeros_like(got))

    x_all = ctx_gather(block_input, 0, fast)
    if fast:
        table = jnp.asarray(blocks.reshape(wa_count, ctx_count, 2))[:, ctx]
        pieces = jnp.stack(
            [
                jnp.concatenate([column_block(qkv_weight, table[g, i]) for i in range(2)], axis=1)
                for g in range(wa_count)
            ]
        )
        piece = wa_exchange(pieces).reshape(width, 2 * HEAD_DIM)
        group_weight = ctx_gather(piece, 1, fast)
    else:
        zero_block = jnp.zeros((qkv_weight.shape[0], HEAD_DIM), bf16)

        def static_block(b):
            if b == none:
                return zero_block
            return qkv_weight[:, b * HEAD_DIM : (b + 1) * HEAD_DIM]

        pieces = jnp.stack(
            [jnp.concatenate([static_block(b) for b in blocks[g]], axis=1) for g in range(wa_count)]
        )
        group_weight = lax.all_to_all(pieces, "wa", 0, 0).reshape(width, slots * HEAD_DIM)

    zero_rows = jnp.zeros((HEAD_DIM, col_width), bf16)
    turned = jnp.concatenate(
        [
            out_weight[h * HEAD_DIM : (h + 1) * HEAD_DIM] if h >= 0 else zero_rows
            for h in heads_flat
        ]
    )
    if fast:
        part = turned.shape[0] // ctx_count
        turned = lax.dynamic_slice_in_dim(turned, ctx * part, part, 0)
        out_full = ctx_gather(wa_gather(turned, 1), 0, fast)
    else:
        out_full = lax.all_gather(turned, "wa", axis=1, tiled=True)

    bias_blocks = jnp.concatenate(
        [
            query_bias.reshape(HEADS, HEAD_DIM),
            jnp.zeros((HEADS, HEAD_DIM), f32),
            value_bias.reshape(HEADS, HEAD_DIM),
            jnp.zeros((1, HEAD_DIM), f32),
        ]
    )
    chosen = (jnp.asarray(blocks)[wa][:, None] == jnp.arange(none + 1)[None, :]).astype(f32)
    group_bias = jnp.sum(chosen[:, :, None] * bias_blocks[None], axis=1).reshape(-1)

    normed_all = norm_parts(x_all.astype(f32), attn_gain, attn_shift)[2].astype(bf16)
    qkv_all = (dot(normed_all, group_weight) + group_bias).astype(bf16)
    attn_out, log_norm = call(
        functools.partial(attend_kernel, per),
        (own_ctx,),
        (own_cols, where_row, qkv_all),
        (
            jax.ShapeDtypeStruct((rows, group_width), bf16),
            jax.ShapeDtypeStruct((rows, per), f32),
        ),
        "attend",
    )
    attn_full = wa_gather(attn_out, 1)

    input_f = block_input.astype(f32)
    resid = input_f + dot(attn_full, out_full) + out_bias
    mlp_hat, mlp_inv, mlp_norm = norm_parts(resid, mlp_gain, mlp_shift)
    normed_mid = mlp_norm.astype(bf16)
    hidden_pre = dot(normed_mid, up_weight) + up_bias
    hidden_grad = dot(cotangent, down_weight, 1, 1) * gelu_slope(hidden_pre)
    hidden_grad_b = hidden_grad.astype(bf16)
    mid_part = dot(hidden_grad_b, up_weight, 1, 1)
    mid_grad = wa_scatter(mid_part.astype(bf16).reshape(wa_count, part_rows, width))

    hidden_act = gelu_value(hidden_pre).astype(bf16)
    down_part = dot(hidden_act, down_weight).astype(bf16)
    down_cols = wa_scatter(
        jnp.stack([down_part[:, i * col_width : (i + 1) * col_width] for i in range(wa_count)])
    )
    col_start = wa * col_width
    block_output = (
        lax.dynamic_slice_in_dim(resid + down_bias, col_start, col_width, 1) + down_cols
    ).astype(bf16)

    first = wa * part_rows

    def share(values):
        return lax.dynamic_slice_in_dim(values, first, part_rows, 0)

    grad_share = share(cotangent).astype(f32)
    hat_share = share(mlp_hat)
    resid_grad = grad_share + norm_back(mid_grad, hat_share, share(mlp_inv), mlp_gain)
    resid_grad_b = wa_gather(resid_grad.astype(bf16), 0)
    pack = call(
        functools.partial(grads_kernel, per),
        (own_wa,),
        (resid_grad_b, out_full, attn_out, log_norm),
        jax.ShapeDtypeStruct((rows, -(-(group_width + 4 * per) // 128) * 128), bf16),
        "grads",
    )
    pack_all = ctx_gather(pack, 0, fast)
    query_grad = call(
        functools.partial(query_back_kernel, per),
        (own_ctx,),
        (own_cols, where_row, qkv_all, pack),
        jax.ShapeDtypeStruct((rows, group_width), bf16),
        "query_back",
    )
    key_grad, value_grad = call(
        functools.partial(key_back_kernel, per),
        (own_ctx,),
        (own_cols, where_row, qkv_all, pack_all),
        (
            jax.ShapeDtypeStruct((rows, group_width), bf16),
            jax.ShapeDtypeStruct((rows, group_width), bf16),
        ),
        "key_back",
    )
    pads = slots * HEAD_DIM - 3 * group_width
    pieces = [query_grad, key_grad, value_grad]
    if pads:
        pieces.append(jnp.zeros((rows, pads), bf16))
    qkv_grad_own = jnp.concatenate(pieces, axis=1)

    normed_part = dot(qkv_grad_own, group_weight, 1, 1)
    normed_grad = wa_scatter(normed_part.astype(bf16).reshape(wa_count, part_rows, width))
    attn_hat, attn_inv, _ = norm_parts(input_f, attn_gain, attn_shift)
    input_grad = wa_gather(
        (
            resid_grad + norm_back(normed_grad, share(attn_hat), share(attn_inv), attn_gain)
        ).astype(bf16),
        0,
    )

    def chunk_rows(values):
        return values.astype(bf16).reshape((ctx_count, width // ctx_count) + values.shape[1:])

    up_grad = ctx_scatter(chunk_rows(dot(normed_mid, hidden_grad_b, 0, 0)), fast)
    down_grad = ctx_scatter(chunk_rows(dot(cotangent, hidden_act, 0, 0)), fast).T
    grad_cols = lax.dynamic_slice_in_dim(resid_grad_b, col_start, col_width, 1)
    slot_of = {h: i for i, h in enumerate(heads_flat) if h >= 0}
    out_part = dot(attn_full, grad_cols, 0, 0)
    out_part = jnp.concatenate(
        [out_part[slot_of[h] * HEAD_DIM : (slot_of[h] + 1) * HEAD_DIM] for h in range(HEADS)]
    )
    out_grad = ctx_scatter(chunk_rows(out_part), fast)

    chunk = 3 * width // ctx_count
    if fast:
        sends = np.full((wa_count, ctx_count, 2), slots - 1, np.int32)
        order = np.zeros((ctx_count, 8), np.int32)
        span = 0
        for c in range(ctx_count):
            used = [0] * wa_count
            first_block, last_block = c * chunk // HEAD_DIM, (c * chunk + chunk - 1) // HEAD_DIM
            span = max(span, last_block - first_block + 1)
            for b in range(first_block, last_block + 1):
                g = next(g for g in range(wa_count) if b % HEADS in lists[g])
                sends[g, c, used[g]] = (b // HEADS) * per + lists[g].index(b % HEADS)
                order[c, b - first_block] = 2 * g + used[g]
                used[g] += 1
        by_block = jnp.stack(
            [qkv_grad_own[:, i * HEAD_DIM : (i + 1) * HEAD_DIM] for i in range(slots)]
        )
        mine = jnp.asarray(sends)[wa]
        outgoing = jnp.stack(
            [
                jnp.concatenate(
                    [lax.dynamic_index_in_dim(by_block, mine[c, i], 0, False) for i in range(2)],
                    axis=1,
                )
                for c in range(ctx_count)
            ]
        )
        columns = ctx_exchange(outgoing, fast).reshape(tokens, 2 * HEAD_DIM)
        found = dot(normed_all, columns, 0, 0).astype(bf16)
        found = wa_exchange(found.reshape(wa_count, col_width, 2 * HEAD_DIM))
        halves = jnp.stack(
            [
                found[g, :, i * HEAD_DIM : (i + 1) * HEAD_DIM]
                for g in range(wa_count)
                for i in range(2)
            ]
        )
        mine = jnp.asarray(order)[ctx]
        line = jnp.concatenate(
            [lax.dynamic_index_in_dim(halves, mine[j], 0, False) for j in range(span)], axis=1
        )
        qkv_grad = lax.dynamic_slice_in_dim(line, ctx * chunk % HEAD_DIM, chunk, 1).astype(f32)
    else:
        spread = lax.all_gather(qkv_grad_own, "wa", axis=0, tiled=False)
        parts = []
        for b in range(3 * HEADS):
            g = next(g for g in range(wa_count) if b % HEADS in lists[g])
            i = (b // HEADS) * per + lists[g].index(b % HEADS)
            parts.append(spread[g][:, i * HEAD_DIM : (i + 1) * HEAD_DIM])
        qkv_grad_full = jnp.concatenate(parts, axis=1)
        normed_own = lax.dynamic_slice_in_dim(normed_all, ctx * rows, rows, 0)
        normed_cols = lax.dynamic_slice_in_dim(normed_own, col_start, col_width, 1)
        qkv_grad = lax.psum_scatter(
            dot(normed_cols, qkv_grad_full, 0, 0), "ctx", scatter_dimension=1, tiled=True
        )

    early = jnp.stack(
        [
            jnp.sum(mid_grad * hat_share, axis=0),
            jnp.sum(mid_grad, axis=0),
            jnp.sum(resid_grad, axis=0),
            jnp.sum(grad_share, axis=0),
        ]
    )
    up_sum = jnp.sum(hidden_grad, axis=0).reshape(-1, width)
    early = ctx_sum(jnp.concatenate([early, up_sum]), fast)
    up_bias_grad = early[4:].reshape(-1)
    early = wa_sum(early[:4])
    col_sums = jnp.sum(qkv_grad_own.astype(f32), axis=0).reshape(slots, HEAD_DIM)
    all_sums = jnp.sum(chosen[:, :, None] * col_sums[:, None, :], axis=0)
    late = jnp.stack(
        [
            jnp.sum(normed_part * attn_hat, axis=0),
            jnp.sum(normed_part, axis=0),
            all_sums[:HEADS].reshape(-1),
            all_sums[2 * HEADS : 3 * HEADS].reshape(-1),
        ]
    )
    late = wa_sum(ctx_sum(late, fast))
    return (
        block_output,
        input_grad,
        qkv_grad,
        late[2],
        late[3],
        out_grad,
        early[2],
        up_grad,
        up_bias_grad,
        down_grad,
        early[3],
        late[0],
        late[1],
        early[0],
        early[1],
    )


def solution(mesh):
    fast = mesh.shape["ctx"] == 8 and group_heads(mesh.shape["wa"], 8) is not None
    fast = fast and 3 * -(-HEADS // mesh.shape["wa"]) < 16
    placed = (
        P("ctx", None),
        P(),
        P(),
        P(),
        P(),
        P("wa", None),
        P(),
        P(),
        P(None, "wa"),
        P(),
        P(),
        P(),
        P(None, "wa"),
        P("wa"),
        P("wa", None),
        P(),
        P("ctx", None),
    )
    return jax.shard_map(
        body_eight if fast else functools.partial(body, False),
        mesh=mesh,
        in_specs=placed,
        out_specs=(
            P("ctx", "wa"),
            P("ctx", None),
            P("wa", "ctx"),
            P(),
            P(),
            P("ctx", "wa"),
            P(),
            P("ctx", "wa"),
            P("wa"),
            P("wa", "ctx"),
            P(),
            P(),
            P(),
            P(),
            P(),
        ),
        check_vma=False,
    )
```
